256 devices in a mesh: layer: 4 (over z_hi, core), doc: 64 (over y, x, z_lo).
Axes of the slice: x: 4, y: 4, z: 8 (z_hi: 2, z_lo: 4; z = z_hi * 4 + z_lo), core: 2. Of those that a mesh axis runs over, the one named last changes fastest.
Arguments:
- query_grads: bfloat16 [4, 256, 4096], P('layer', 'doc'), may hold values from -6 to 6
- stored_grads: bfloat16 [4, 65536, 4096], P('layer', 'doc'), may hold values from -0.0234375 to 0.0234375
- basis_in: float32 [4, 64, 64], P('layer'), may hold values from -0.75 to 0.75
- basis_out: float32 [4, 64, 64], P('layer'), may hold values from -0.75 to 0.75
- eigen_values: float32 [4, 64, 64], P('layer'), may hold values from 0.02 to 4
- layer_mask: int32 [256, 4], P(None, 'layer'), may hold values 0 or 1
- doc_counts: int32 [64], P('doc'), may hold values from 1 to 1024, 32768 in all
Outputs:
- scores: float32 [256, 65536], P('layer', 'doc')
The draws below stay inside these ranges and needn't reach their ends.
Inputs may be any that keep to these rules, and one draw needn't show every extreme that they name: `doc_counts`: the counts sum to 32768 and the largest equals 1024.
All inputs are finite; a program needn't handle non-finite values. No bound on the sum of `layer_mask` or of `doc_counts` on one device may be relied on, other than what follows from the above.
Results may differ from the reference program's by a relative error of at most 0.0029.
Values may be sent and summed in bfloat16 or wider, within the bound.
No kernel may reach another device: no remote copies, remote signals or barrier semaphores. Data moves between devices by JAX's collectives and lax.ppermute only.
A program may use at most 64 MiB of HBM per device.

```python
import math
import jax
import jax.numpy as jnp
import numpy as np
from jax import lax

A = 64
B = 64
Q = 256
DOC_DEV = 1024
LAYERS = 4
DOC_SHARDS = 64
DOCS = 65536
N_DOC = 64


def touch_ends(array, stream_key, low, largest):
    shape = array.shape
    spot = [jax.random.randint(jax.random.fold_in(stream_key, axis), (), 0, shape[axis]) for axis in range(len(shape))]
    array = array.at[tuple(spot)].set(low)
    longest = shape.index(max(shape))
    spot[longest] = (spot[longest] + 1) % shape[longest]
    return array.at[tuple(spot)].set(largest)


def steps_of(rng, dims, shards, smallest, high):
    def one(dim, parts):
        draws = jax.random.uniform(jax.random.fold_in(jax.random.fold_in(rng, 6), dim), (parts,), jnp.float32, smallest / len(shards), high / len(shards))
        return jnp.repeat(jnp.exp(draws), dims[dim] // parts).reshape((-1,) + (1,) * (len(dims) - dim - 1))

    factor_of = one(*shards[0])
    for cut in shards[1:]:
        factor_of = factor_of * one(*cut)
    return factor_of


def length_profile(amount, total, most, skew):
    portions = [(1 << 20) // math.isqrt(standing ** skew) + 1 for standing in range(2, amount + 1)]
    rest, given = total - most - (amount - 1), [1] * (amount - 1)
    while rest > 0:
        candidates = [i for i in range(amount - 1) if given[i] < most]
        mass, remaining = sum([portions[i] for i in candidates]), rest
        for i in candidates:
            addition = min(most - given[i], max(1, remaining * portions[i] // mass), rest)
            given[i] = given[i] + addition
            rest = rest - addition
    return np.array([most] + given)


def ragged_sizes(key, amount, total, reach, skew):
    if amount == 2:
        one = jax.random.randint(key, (), max(1, total - reach), min(reach, total - 1) + 1)
        return jnp.stack([one, total - one])
    tallies = jnp.asarray(length_profile(amount, total, reach, skew), jnp.int32)
    twos = (amount - 1) // 2
    giver, receiver = tallies[1:1 + 2 * twos:2], tallies[2:2 + 2 * twos:2]
    slack = jnp.minimum(giver - 1, reach - receiver)
    shifted = jax.random.randint(jax.random.fold_in(key, 1), (twos,), 0, 1 << 20) % (slack + 1)
    tallies = tallies.at[1:1 + 2 * twos:2].set(giver - shifted).at[2:2 + 2 * twos:2].set(receiver + shifted)
    return tallies[jax.random.permutation(jax.random.fold_in(key, 2), amount)]


def bell_draw(own_key, shape, spread, reach, pieces=(), kind=jnp.bfloat16):
    values = spread * jax.random.normal(own_key, shape, jnp.float32)
    if pieces:
        values = values * steps_of(own_key, shape, pieces, -0.22, 0.18)
    return jnp.clip(values, -reach, reach).astype(kind)


def setup_inputs(seed: int = 0) -> dict:
    keys = jax.random.split(jax.random.key(seed), 8)
    query_grads = bell_draw(keys[0], (LAYERS, Q, B * A), 1.0, 6.0, ((0, 4), (1, 64)))
    stored_grads = bell_draw(keys[1], (LAYERS, DOCS, B * A), (16 * B * A) ** -0.5, 0.0234375, ((0, 4), (1, 64)))
    basis_in = bell_draw(keys[2], (LAYERS, A, A), A ** -0.5, 0.75, ((0, 4),), jnp.float32)
    basis_out = bell_draw(keys[3], (LAYERS, B, B), B ** -0.5, 0.75, ((0, 4),), jnp.float32)
    eigen_values = jnp.clip(jnp.exp(math.log(4.0) - 5.2983174 * jax.random.uniform(keys[4], (LAYERS, B, A), jnp.float32) ** steps_of(keys[4], (LAYERS, B, A), ((0, 4),), -0.2, 0.2)), 0.02, 4.0)
    layer_mask = touch_ends((jax.random.randint(keys[5], (Q, LAYERS), 0, 4) < 3).astype(jnp.int32), jax.random.fold_in(keys[5], 1), 0, 1)
    doc_counts = ragged_sizes(keys[6], DOC_SHARDS, DOC_DEV * N_DOC // 2, DOC_DEV, 2).astype(jnp.int32)
    return {"query_grads": query_grads, "stored_grads": stored_grads, "basis_in": basis_in, "basis_out": basis_out, "eigen_values": eigen_values, "layer_mask": layer_mask, "doc_counts": doc_counts}


damping = 0.1


def precondition(gradients, basis_in, basis_out, eigen_values):
    row_count = gradients.shape[0]
    grid_blocks = gradients.astype(jnp.float32).reshape(row_count, basis_out.shape[0], basis_in.shape[0])
    rotated = jnp.einsum("xi,qxy,yj->qij", basis_out, grid_blocks, basis_in, precision=lax.Precision.HIGHEST)
    scaled = rotated / (eigen_values + damping)
    restored = jnp.einsum("bi,qij,aj->qba", basis_out, scaled, basis_in, precision=lax.Precision.HIGHEST)
    return restored.reshape(row_count, -1).astype(jnp.bfloat16)


def reference(query_grads, stored_grads, basis_in, basis_out, eigen_values, layer_mask, doc_counts):
    live_slots = (jnp.arange(DOC_DEV, dtype=jnp.int32)[None, :] < doc_counts[:, None]).reshape(-1)

    def one_layer(carry, inputs):
        queries, stored, base_in, base_out, eigens, weights = inputs
        prepared = precondition(queries, base_in, base_out, eigens)
        prepared = prepared * weights.astype(prepared.dtype)[:, None]
        tile = lax.dot_general(prepared, stored, (((1,), (1,)), ((), ())), preferred_element_type=jnp.float32)
        return carry + tile, None

    start_value = jnp.zeros((Q, DOCS), jnp.float32)
    summed, _ = lax.scan(one_layer, start_value, (query_grads, stored_grads, basis_in, basis_out, eigen_values, layer_mask.T))
    return jnp.where(live_slots[None, :], summed, jnp.zeros_like(summed))
```

```python
import jax
import jax.numpy as jnp
from jax import lax
from jax.sharding import PartitionSpec as P

damping = 0.1

side = 4


def doc_pairs(stride, flip):
    return [(d, d ^ (flip * stride)) for d in range(side**3)]


def layer_pairs(flip):
    return [(l, l ^ flip) for l in range(4)]


def precondition(gradients, basis_in, basis_out, eigen_values):
    row_count = gradients.shape[0]
    grid_blocks = gradients.astype(jnp.float32).reshape(
        row_count, basis_out.shape[0], basis_in.shape[0]
    )
    rotated = jnp.einsum(
        "xi,qxy,yj->qij", basis_out, grid_blocks, basis_in, precision=lax.Precision.HIGHEST
    )
    scaled = rotated / (eigen_values + damping)
    restored = jnp.einsum(
        "bi,qij,aj->qba", basis_out, scaled, basis_in, precision=lax.Precision.HIGHEST
    )
    return restored.reshape(row_count, -1).astype(jnp.bfloat16)


def fetch(block, stride):
    return [block] + [lax.ppermute(block, "doc", doc_pairs(stride, k)) for k in (1, 3, 2)]


def by_flip(blocks):
    own, one, three, two = blocks
    return [own, one, two, three]


def ordered(blocks, coordinate):
    low, high = (coordinate & 1) == 1, (coordinate & 2) == 2
    a, b, c, d = blocks
    a, b, c, d = (jnp.where(low, p, q) for p, q in ((b, a), (a, b), (d, c), (c, d)))
    return [jnp.where(high, p, q) for p, q in ((c, a), (d, b), (a, c), (b, d))]


def on_device(query_grads, stored_grads, basis_in, basis_out, eigen_values, layer_mask, doc_counts):
    doc, layer = lax.axis_index("doc"), lax.axis_index("layer")
    y, x, z = doc // 16, (doc // 4) % 4, doc % 4
    stored = stored_grads[0]
    own = precondition(query_grads[0], basis_in[0], basis_out[0], eigen_values[0])
    weights = lax.dynamic_slice(layer_mask[:, 0], (4 * doc,), (4,)).astype(jnp.bfloat16)
    own = own * weights[:, None]

    rows = ordered(by_flip(fetch(own, 1)), z)
    upper = jnp.concatenate(rows[:2], axis=0)
    lower = jnp.concatenate(rows[2:], axis=0)
    upper, lower = lax.optimization_barrier((upper, lower))
    upper = jnp.stack(by_flip(fetch(upper, 16)))
    lower = jnp.stack(by_flip(fetch(lower, 4)))
    upper = jnp.stack(by_flip(fetch(upper, 4)))
    lower = jnp.stack(by_flip(fetch(lower, 16)))
    queries = jnp.concatenate([upper.reshape(128, 4096), lower.reshape(128, 4096)])

    tiles = lax.dot_general(
        queries, stored, (((1,), (1,)), ((), ())), preferred_element_type=jnp.float32
    )
    slots = stored.shape[0]
    upper = tiles[:128].reshape(4, 4, 8, slots).transpose(1, 0, 2, 3)
    lower = tiles[128:].reshape(4, 4, 8, slots)
    tiles = jnp.stack([upper, lower], axis=1)
    tiles = tiles.reshape(2, 2, 2, 4, 8, slots)
    core, far = layer & 1, layer >> 1
    keep = (y & 1) ^ core
    mine = lax.dynamic_index_in_dim(tiles, keep, 1, keepdims=False)
    give = lax.dynamic_index_in_dim(tiles, 1 - keep, 1, keepdims=False)
    pair = mine + lax.ppermute(give, "layer", layer_pairs(1))
    keep = (y >> 1) ^ far
    mine = lax.dynamic_index_in_dim(pair, keep, 0, keepdims=False)
    give = lax.dynamic_index_in_dim(pair, 1 - keep, 0, keepdims=False)
    total = mine + lax.ppermute(give, "layer", layer_pairs(2))
    total = jnp.stack(ordered([total[:, k] for k in range(4)], x))
    total = total.reshape(64, slots)
    live_slots = jnp.arange(slots, dtype=jnp.int32) < doc_counts[0]
    return jnp.where(live_slots[None, :], total, jnp.zeros_like(total))


def solution(mesh):
    in_specs = (
        P("layer", "doc", None),
        P("layer", "doc", None),
        P("layer", None, None),
        P("layer", None, None),
        P("layer", None, None),
        P(None, "layer"),
        P("doc"),
    )
    out_specs = P("layer", "doc")
    return jax.shard_map(
        on_device, mesh=mesh, in_specs=in_specs, out_specs=out_specs, check_vma=False
    )
```

```python
import jax
import jax.numpy as jnp
from jax import lax
from jax.experimental import pallas as pl
from jax.experimental.pallas import tpu as pltpu
from jax.sharding import PartitionSpec as P

damping = 0.1

side = 4


def doc_pairs(stride, flip):
    return [(d, d ^ (flip * stride)) for d in range(side**3)]


def layer_pairs(flip):
    return [(l, l ^ flip) for l in range(4)]


def exact_dot(a, b, dims):
    return lax.dot_general(
        a, b, (dims, ((), ())), precision=lax.Precision.HIGHEST, preferred_element_type=jnp.float32
    )


def precondition_kernel(mask_ref, doc_ref, grads_ref, basis_in_ref, basis_out_ref, eigen_ref, out_ref):
    count, out_size, in_size = grads_ref.shape[0], basis_out_ref.shape[0], basis_in_ref.shape[0]
    base_in, base_out = basis_in_ref[...], basis_out_ref[...]
    divisor = eigen_ref[...] + damping
    grads = grads_ref[...].astype(jnp.float32).reshape(count, out_size, in_size)
    blocks = [grads[q] for q in range(count)]
    side_by_side = exact_dot(base_out, jnp.concatenate(blocks, axis=1), ((0,), (0,)))
    stacked = jnp.concatenate(jnp.split(side_by_side, count, axis=1), axis=0)
    rotated = exact_dot(stacked, base_in, ((1,), (0,)))
    scaled = rotated / jnp.concatenate([divisor] * count, axis=0)
    half = exact_dot(scaled, base_in, ((1,), (1,)))
    side_by_side = jnp.concatenate(jnp.split(half, count, axis=0), axis=1)
    restored = exact_dot(base_out, side_by_side, ((1,), (0,)))
    rows = []
    for q, block in enumerate(jnp.split(restored, count, axis=1)):
        weight = mask_ref[doc_ref[0] * count + q].astype(jnp.float32)
        rows.append(block * weight)
    out_ref[...] = jnp.stack(rows).reshape(count, out_size * in_size).astype(jnp.bfloat16)


def precondition(gradients, basis_in, basis_out, eigen_values, mask, doc):
    vmem, smem = pl.BlockSpec(memory_space=pltpu.VMEM), pl.BlockSpec(memory_space=pltpu.SMEM)
    return pl.pallas_call(
        precondition_kernel,
        out_shape=jax.ShapeDtypeStruct(gradients.shape, jnp.bfloat16),
        in_specs=[smem, smem, vmem, vmem, vmem, vmem],
        out_specs=vmem,
        name="precondition",
    )(mask, doc.reshape(1), gradients, basis_in, basis_out, eigen_values)


def score_kernel(queries_ref, stored_ref, out_ref):
    width = 256

    def tile(i, carry):
        columns = pl.ds(pl.multiple_of(i * width, width), width)
        out_ref[:, columns] = lax.dot_general(
            queries_ref[...],
            stored_ref[columns, :],
            (((1,), (1,)), ((), ())),
            preferred_element_type=jnp.float32,
        )
        return carry

    lax.fori_loop(0, stored_ref.shape[0] // width, tile, 0)


def score(queries, stored):
    vmem = pl.BlockSpec(memory_space=pltpu.VMEM)
    rows, slots = queries.shape[0], stored.shape[0]
    return pl.pallas_call(
        score_kernel,
        out_shape=jax.ShapeDtypeStruct((rows, slots), jnp.float32),
        in_specs=[vmem, vmem],
        out_specs=vmem,
        compiler_params=pltpu.CompilerParams(vmem_limit_bytes=8 << 20),
        cost_estimate=pl.CostEstimate(
            flops=2 * rows * slots * stored.shape[1], bytes_accessed=0, transcendentals=0
        ),
        name="score",
    )(queries, stored)


def fetch(block, stride):
    return [block] + [lax.ppermute(block, "doc", doc_pairs(stride, k)) for k in (1, 3, 2)]


def by_flip(blocks):
    own, one, three, two = blocks
    return [own, one, two, three]


def ordered(blocks, coordinate):
    low, high = (coordinate & 1) == 1, (coordinate & 2) == 2
    a, b, c, d = blocks
    a, b, c, d = (jnp.where(low, p, q) for p, q in ((b, a), (a, b), (d, c), (c, d)))
    return [jnp.where(high, p, q) for p, q in ((c, a), (d, b), (a, c), (b, d))]


def on_device(query_grads, stored_grads, basis_in, basis_out, eigen_values, layer_mask, doc_counts):
    doc, layer = lax.axis_index("doc"), lax.axis_index("layer")
    y, x, z = doc // 16, (doc // 4) % 4, doc % 4
    stored = pltpu.with_memory_space_constraint(stored_grads[0], pltpu.VMEM)
    own = precondition(
        query_grads[0], basis_in[0], basis_out[0], eigen_values[0], layer_mask[:, 0], doc
    )

    rows = ordered(by_flip(fetch(own, 1)), z)
    upper = jnp.concatenate(rows[:2], axis=0)
    lower = jnp.concatenate(rows[2:], axis=0)
    upper, lower = lax.optimization_barrier((upper, lower))
    upper = jnp.stack(by_flip(fetch(upper, 16)))
    lower = jnp.stack(by_flip(fetch(lower, 4)))
    upper = jnp.stack(by_flip(fetch(upper, 4)))
    lower = jnp.stack(by_flip(fetch(lower, 16)))
    queries = jnp.concatenate([upper.reshape(128, 4096), lower.reshape(128, 4096)])

    tiles = score(queries, stored)
    slots = stored.shape[0]
    upper = tiles[:128].reshape(4, 4, 8, slots).transpose(1, 0, 2, 3)
    lower = tiles[128:].reshape(4, 4, 8, slots)
    tiles = jnp.stack([upper, lower], axis=1)
    tiles = tiles.reshape(2, 2, 2, 4, 8, slots)
    core, far = layer & 1, layer >> 1
    keep = (y & 1) ^ core
    mine = lax.dynamic_index_in_dim(tiles, keep, 1, keepdims=False)
    give = lax.dynamic_index_in_dim(tiles, 1 - keep, 1, keepdims=False)
    pair = mine + lax.ppermute(give, "layer", layer_pairs(1))
    keep = (y >> 1) ^ far
    mine = lax.dynamic_index_in_dim(pair, keep, 0, keepdims=False)
    give = lax.dynamic_index_in_dim(pair, 1 - keep, 0, keepdims=False)
    other = lax.ppermute(give.astype(jnp.bfloat16), "layer", layer_pairs(2))
    total = mine + other.astype(jnp.float32)
    total = jnp.stack(ordered([total[:, k] for k in range(4)], x))
    total = total.reshape(64, slots)
    live_slots = jnp.arange(slots, dtype=jnp.int32) < doc_counts[0]
    return jnp.where(live_slots[None, :], total, jnp.zeros_like(total))


def solution(mesh):
    in_specs = (
        P("layer", "doc", None),
        P("layer", "doc", None),
        P("layer", None, None),
        P("layer", None, None),
        P("layer", None, None),
        P(None, "layer"),
        P("doc"),
    )
    out_specs = P("layer", "doc")
    return jax.shard_map(
        on_device, mesh=mesh, in_specs=in_specs, out_specs=out_specs, check_vma=False
    )
```

```python
import functools

import jax
import jax.numpy as jnp
from jax import lax
from jax.experimental import pallas as pl
from jax.experimental.pallas import tpu as pltpu
from jax.sharding import PartitionSpec as P

damping = 0.1

side = 4


def doc_pairs(stride, flip):
    return [(d, d ^ (flip * stride)) for d in range(side**3)]


def layer_pairs(flip):
    return [(l, l ^ flip) for l in range(4)]


def exact_dot(a, b, dims):
    return lax.dot_general(
        a, b, (dims, ((), ())), precision=lax.Precision.HIGHEST, preferred_element_type=jnp.float32
    )


def precondition_kernel(mask_ref, doc_ref, grads_ref, basis_in_ref, basis_out_ref, eigen_ref, out_ref):
    count, out_size, in_size = grads_ref.shape[0], basis_out_ref.shape[0], basis_in_ref.shape[0]
    base_in, base_out = basis_in_ref[...], basis_out_ref[...]
    divisor = eigen_ref[...] + damping
    grads = grads_ref[...].astype(jnp.float32).reshape(count, out_size, in_size)
    blocks = [grads[q] for q in range(count)]
    side_by_side = exact_dot(base_out, jnp.concatenate(blocks, axis=1), ((0,), (0,)))
    stacked = jnp.concatenate(jnp.split(side_by_side, count, axis=1), axis=0)
    rotated = exact_dot(stacked, base_in, ((1,), (0,)))
    scaled = rotated / jnp.concatenate([divisor] * count, axis=0)
    half = exact_dot(scaled, base_in, ((1,), (1,)))
    side_by_side = jnp.concatenate(jnp.split(half, count, axis=0), axis=1)
    restored = exact_dot(base_out, side_by_side, ((1,), (0,)))
    rows = []
    for q, block in enumerate(jnp.split(restored, count, axis=1)):
        weight = mask_ref[doc_ref[0] * count + q].astype(jnp.float32)
        rows.append(block * weight)
    out_ref[...] = jnp.stack(rows).reshape(count, out_size * in_size).astype(jnp.bfloat16)


def precondition(gradients, basis_in, basis_out, eigen_values, mask, doc):
    vmem, smem = pl.BlockSpec(memory_space=pltpu.VMEM), pl.BlockSpec(memory_space=pltpu.SMEM)
    operands = [
        pltpu.with_memory_space_constraint(a, pltpu.HBM)
        for a in (mask, gradients, basis_in, basis_out, eigen_values)
    ]
    return pl.pallas_call(
        precondition_kernel,
        out_shape=jax.ShapeDtypeStruct(gradients.shape, jnp.bfloat16),
        in_specs=[smem, smem, vmem, vmem, vmem, vmem],
        out_specs=vmem,
        compiler_params=pltpu.CompilerParams(vmem_limit_bytes=4 << 20),
        name="precondition",
    )(operands[0], doc.reshape(1), *operands[1:])


straight = (
    [(0, 0, h) for h in range(2)]
    + [(0, k, h) for k in (1, 2, 3) for h in range(2)]
    + [(k, 0, h) for k in (1, 2, 3) for h in range(2)]
)
diagonal = [(j, i, 0) for i in (1, 2, 3) for j in (1, 2, 3)] + [
    (j, i, 1) for j in (1, 2, 3) for i in (1, 2, 3)
]


def place_kernel(tiles, place_ref, *refs):
    out_ref = refs[-1]
    core_row, far_row, x = place_ref[0], place_ref[1], place_ref[2]
    t = 0
    for piece in refs:
        if t == len(tiles):
            break
        for row in range(0, piece.shape[0], 8):
            ky, kx, half = tiles[t]
            out_ref[core_row ^ (ky & 1), far_row ^ (ky >> 1), x ^ kx, half] = piece[row : row + 8]
            t += 1


def placed(tiles, place, pieces, flops, begun=None):
    vmem, smem = pl.BlockSpec(memory_space=pltpu.VMEM), pl.BlockSpec(memory_space=pltpu.SMEM)
    width = pieces[0].shape[1]
    operands = pieces + ([] if begun is None else [begun])
    return pl.pallas_call(
        functools.partial(place_kernel, tiles),
        out_shape=jax.ShapeDtypeStruct((2, 2, 4, 2, 8, width), jnp.bfloat16),
        in_specs=[smem] + [vmem] * len(operands),
        out_specs=vmem,
        input_output_aliases={} if begun is None else {len(operands): 0},
        compiler_params=pltpu.CompilerParams(vmem_limit_bytes=8 << 20),
        cost_estimate=pl.CostEstimate(flops=flops, bytes_accessed=0, transcendentals=0),
        name="placed",
    )(place, *operands)


def score_kernel(queries_ref, stored_ref, out_ref):
    width = 256

    def tile(i, carry):
        columns = pl.ds(pl.multiple_of(i * width, width), width)
        out_ref[:, columns] = lax.dot_general(
            queries_ref[...],
            stored_ref[columns, :],
            (((1,), (1,)), ((), ())),
            preferred_element_type=jnp.float32,
        )
        return carry

    lax.fori_loop(0, stored_ref.shape[0] // width, tile, 0)


def score(queries, stored):
    vmem = pl.BlockSpec(memory_space=pltpu.VMEM)
    rows, slots = queries.shape[0], stored.shape[0]
    return pl.pallas_call(
        score_kernel,
        out_shape=jax.ShapeDtypeStruct((rows, slots), jnp.float32),
        in_specs=[vmem, vmem],
        out_specs=vmem,
        compiler_params=pltpu.CompilerParams(vmem_limit_bytes=8 << 20),
        cost_estimate=pl.CostEstimate(
            flops=2 * queries.size * slots, bytes_accessed=0, transcendentals=0
        ),
        name="score",
    )(queries, stored)


def fetch(block, stride):
    blocks = []
    for k in (1, 2, 3):
        blocks.append(lax.ppermute(block, "doc", doc_pairs(stride, k)))
    return blocks


def ordered(blocks, coordinate):
    low, high = (coordinate & 1) == 1, (coordinate & 2) == 2
    a, b, c, d = blocks
    a, b, c, d = (jnp.where(low, p, q) for p, q in ((b, a), (a, b), (d, c), (c, d)))
    return [jnp.where(high, p, q) for p, q in ((c, a), (d, b), (a, c), (b, d))]


def on_device(query_grads, stored_grads, basis_in, basis_out, eigen_values, layer_mask, doc_counts):
    doc, layer = lax.axis_index("doc"), lax.axis_index("layer")
    y, x, z = doc // 16, (doc // 4) % 4, doc % 4
    stored = pltpu.with_memory_space_constraint(stored_grads[0], pltpu.VMEM)
    own = precondition(
        query_grads[0], basis_in[0], basis_out[0], eigen_values[0], layer_mask[:, 0], doc
    )

    rows = ordered([own] + fetch(own, 1), z)
    block = lax.optimization_barrier(jnp.concatenate(rows, axis=0))
    along_y, along_x = fetch(block, 16), fetch(block, 4)
    core, far = layer & 1, layer >> 1
    place = jnp.stack([(y & 1) ^ core, (y >> 1) ^ far, x]).astype(jnp.int32)
    queries = placed(straight, place, [block] + along_x + along_y, 2 * 10**10)
    upper = jnp.concatenate([b[:8] for b in along_y])
    lower = jnp.concatenate([b[8:] for b in along_x])
    diagonals = fetch(upper, 4) + fetch(lower, 16)
    queries = placed(diagonal, place, diagonals, 10**8, queries)
    tiles = score(queries.reshape(256, -1), stored)
    tiles = tiles.reshape(2, 2, 4, 2, 8, -1)
    other = lax.ppermute(tiles[1], "layer", layer_pairs(1))
    give = (tiles[0, 1] + other[1]).astype(jnp.bfloat16)
    other_far = lax.ppermute(give, "layer", layer_pairs(2))
    total = tiles[0, 0] + other[0] + other_far.astype(jnp.float32)
    slots = stored.shape[0]
    total = total.reshape(64, slots)
    live_slots = jnp.arange(slots, dtype=jnp.int32) < doc_counts[0]
    return jnp.where(live_slots[None, :], total, jnp.zeros_like(total))


def solution(mesh):
    in_specs = (
        P("layer", "doc", None),
        P("layer", "doc", None),
        P("layer", None, None),
        P("layer", None, None),
        P("layer", None, None),
        P(None, "layer"),
        P("doc"),
    )
    out_specs = P("layer", "doc")
    return jax.shard_map(
        on_device, mesh=mesh, in_specs=in_specs, out_specs=out_specs, check_vma=False
    )
```

```python
import functools

import jax
import jax.numpy as jnp
from jax import lax
from jax.experimental import pallas as pl
from jax.experimental.pallas import tpu as pltpu
from jax.sharding import PartitionSpec as P

damping = 0.1

side = 4


def doc_pairs(stride, flip):
    return [(d, d ^ (flip * stride)) for d in range(side**3)]


def layer_pairs(flip):
    return [(l, l ^ flip) for l in range(4)]


def exact_dot(a, b, dims):
    return lax.dot_general(
        a, b, (dims, ((), ())), precision=lax.Precision.HIGHEST, preferred_element_type=jnp.float32
    )


def precondition_kernel(mask_ref, doc_ref, grads_ref, basis_in_ref, basis_out_ref, eigen_ref, out_ref):
    count, out_size, in_size = grads_ref.shape[0], basis_out_ref.shape[0], basis_in_ref.shape[0]
    base_in, base_out = basis_in_ref[...], basis_out_ref[...]
    divisor = eigen_ref[...] + damping
    grads = grads_ref[...].astype(jnp.float32).reshape(count, out_size, in_size)
    blocks = [grads[q] for q in range(count)]
    side_by_side = exact_dot(base_out, jnp.concatenate(blocks, axis=1), ((0,), (0,)))
    stacked = jnp.concatenate(jnp.split(side_by_side, count, axis=1), axis=0)
    rotated = exact_dot(stacked, base_in, ((1,), (0,)))
    scaled = rotated / jnp.concatenate([divisor] * count, axis=0)
    half = exact_dot(scaled, base_in, ((1,), (1,)))
    side_by_side = jnp.concatenate(jnp.split(half, count, axis=0), axis=1)
    restored = exact_dot(base_out, side_by_side, ((1,), (0,)))
    rows = []
    for q, block in enumerate(jnp.split(restored, count, axis=1)):
        weight = mask_ref[doc_ref[0] * count + q].astype(jnp.float32)
        rows.append(block * weight)
    out_ref[...] = jnp.stack(rows).reshape(count, out_size * in_size).astype(jnp.bfloat16)


def precondition(gradients, basis_in, basis_out, eigen_values, mask, doc):
    vmem, smem = pl.BlockSpec(memory_space=pltpu.VMEM), pl.BlockSpec(memory_space=pltpu.SMEM)
    operands = [
        pltpu.with_memory_space_constraint(a, pltpu.HBM)
        for a in (mask, gradients, basis_in, basis_out, eigen_values)
    ]
    return pl.pallas_call(
        precondition_kernel,
        out_shape=jax.ShapeDtypeStruct(gradients.shape, jnp.bfloat16),
        in_specs=[smem, smem, vmem, vmem, vmem, vmem],
        out_specs=vmem,
        compiler_params=pltpu.CompilerParams(vmem_limit_bytes=4 << 20),
        name="precondition",
    )(operands[0], doc.reshape(1), *operands[1:])


straight = (
    [(0, 0, h) for h in range(2)]
    + [(0, k, h) for k in (1, 2, 3) for h in range(2)]
    + [(k, 0, h) for k in (1, 2, 3) for h in range(2)]
)
diagonal = (
    [t for i in (1, 3) for t in ((2, i, 0), (2, i, 1), (1, i, 0), (1, i, 1), (3, i, 0))]
    + [(2, 2, 0), (2, 2, 1), (1, 2, 0), (1, 2, 1)]
    + [(3, 2, 0), (3, 2, 1), (3, 1, 1), (3, 3, 1)]
)


def place_kernel(tiles, *refs):
    out_ref = refs[-1]
    doc, layer = lax.axis_index("doc"), lax.axis_index("layer")
    y, x = doc >> 4, (doc >> 2) & 3
    core_row, far_row = (y ^ layer) & 1, (y >> 1) ^ (layer >> 1)
    t = 0
    for piece in refs:
        if t == len(tiles):
            break
        for row in range(0, piece.shape[0], 8):
            ky, kx, half = tiles[t]
            out_ref[core_row ^ (ky & 1), far_row ^ (ky >> 1), x ^ kx, half] = piece[row : row + 8]
            t += 1


def placed(tiles, pieces, flops, begun=None):
    vmem = pl.BlockSpec(memory_space=pltpu.VMEM)
    width = pieces[0].shape[1]
    operands = pieces + ([] if begun is None else [begun])
    return pl.pallas_call(
        functools.partial(place_kernel, tiles),
        out_shape=jax.ShapeDtypeStruct((2, 2, 4, 2, 8, width), jnp.bfloat16),
        in_specs=[vmem] * len(operands),
        out_specs=vmem,
        input_output_aliases={} if begun is None else {len(operands) - 1: 0},
        compiler_params=pltpu.CompilerParams(vmem_limit_bytes=8 << 20),
        cost_estimate=pl.CostEstimate(flops=flops, bytes_accessed=0, transcendentals=0),
        name="placed",
    )(*operands)


def score_kernel(queries_ref, stored_ref, out_ref):
    width = 256

    def tile(i, carry):
        columns = pl.ds(pl.multiple_of(i * width, width), width)
        out_ref[:, columns] = lax.dot_general(
            queries_ref[...],
            stored_ref[columns, :],
            (((1,), (1,)), ((), ())),
            preferred_element_type=jnp.float32,
        )
        return carry

    lax.fori_loop(0, stored_ref.shape[0] // width, tile, 0)


def score(queries, stored):
    vmem = pl.BlockSpec(memory_space=pltpu.VMEM)
    rows, slots = queries.shape[0], stored.shape[0]
    return pl.pallas_call(
        score_kernel,
        out_shape=jax.ShapeDtypeStruct((rows, slots), jnp.float32),
        in_specs=[vmem, vmem],
        out_specs=vmem,
        compiler_params=pltpu.CompilerParams(vmem_limit_bytes=8 << 20),
        cost_estimate=pl.CostEstimate(
            flops=2 * queries.size * slots, bytes_accessed=0, transcendentals=0
        ),
        name="score",
    )(queries, stored)


def fetch(block, stride, flips=(1, 2, 3)):
    blocks = []
    for k in flips:
        blocks.append(lax.ppermute(block, "doc", doc_pairs(stride, k)))
    return blocks


def ordered(blocks, coordinate):
    low, high = (coordinate & 1) == 1, (coordinate & 2) == 2
    a, b, c, d = blocks
    a, b, c, d = (jnp.where(low, p, q) for p, q in ((b, a), (a, b), (d, c), (c, d)))
    return [jnp.where(high, p, q) for p, q in ((c, a), (d, b), (a, c), (b, d))]


def on_device(query_grads, stored_grads, basis_in, basis_out, eigen_values, layer_mask, doc_counts):
    doc = lax.axis_index("doc")
    z = doc % 4
    stored = pltpu.with_memory_space_constraint(stored_grads[0], pltpu.VMEM)
    own = precondition(
        query_grads[0], basis_in[0], basis_out[0], eigen_values[0], layer_mask[:, 0], doc
    )

    rows = ordered([own] + fetch(own, 1), z)
    block = lax.optimization_barrier(jnp.concatenate(rows, axis=0))
    along_y, along_x = fetch(block, 16), fetch(block, 4)
    queries = placed(straight, [block] + along_x + along_y, 2 * 10**10)
    (y1, y2, y3), (x1, x2, x3) = along_y, along_x
    upper = jnp.concatenate([y2, y1, y3[:8]])
    lower = jnp.concatenate([x2, x1[8:], x3[8:]])
    diagonals = (
        fetch(upper, 4, (1, 3))
        + fetch(y2, 4, (2,))
        + fetch(x2, 16, (1,))
        + fetch(lower, 16, (3,))
    )
    queries = placed(diagonal, diagonals, 10**8, queries)
    tiles = score(queries.reshape(256, -1), stored)
    tiles = tiles.reshape(2, 2, 4, 2, 8, -1)
    other = lax.ppermute(tiles[1], "layer", layer_pairs(1))
    give = (tiles[0, 1] + other[1]).astype(jnp.bfloat16)
    other_far = lax.ppermute(give, "layer", layer_pairs(2))
    total = tiles[0, 0] + other[0] + other_far.astype(jnp.float32)
    slots = stored.shape[0]
    total = total.reshape(64, slots)
    live_slots = jnp.arange(slots, dtype=jnp.int32) < doc_counts[0]
    return jnp.where(live_slots[None, :], total, jnp.zeros_like(total))


def solution(mesh):
    in_specs = (
        P("layer", "doc", None),
        P("layer", "doc", None),
        P("layer", None, None),
        P("layer", None, None),
        P("layer", None, None),
        P(None, "layer"),
        P("doc"),
    )
    out_specs = P("layer", "doc")
    return jax.shard_map(
        on_device, mesh=mesh, in_specs=in_specs, out_specs=out_specs, check_vma=False
    )
```

```python
import functools

import jax
import jax.numpy as jnp
from jax import lax
from jax.experimental import pallas as pl
from jax.experimental.pallas import tpu as pltpu
from jax.sharding import PartitionSpec as P

damping = 0.1

side = 4


def doc_pairs(stride, flip):
    return [(d, d ^ (flip * stride)) for d in range(side**3)]


def layer_pairs(flip):
    return [(l, l ^ flip) for l in range(4)]


def halves(a):
    high = a.astype(jnp.bfloat16)
    return high, (a - high.astype(jnp.float32)).astype(jnp.bfloat16)


def exact_dot(a, b, dims):
    (a_high, a_low), (b_high, b_low) = halves(a), halves(b)
    dot = lambda p, q: lax.dot_general(p, q, (dims, ((), ())), preferred_element_type=jnp.float32)
    return dot(a_high, b_high) + (dot(a_high, b_low) + dot(a_low, b_high))


def precondition_kernel(mask_ref, grads_ref, basis_in_ref, basis_out_ref, eigen_ref, out_ref):
    count, out_size, in_size = grads_ref.shape[0], basis_out_ref.shape[0], basis_in_ref.shape[0]
    base_in, base_out = basis_in_ref[...], basis_out_ref[...]
    divisor = eigen_ref[...] + damping
    grads = grads_ref[...].astype(jnp.float32).reshape(count, out_size, in_size)
    blocks = [grads[q] for q in range(count)]
    side_by_side = exact_dot(base_out, jnp.concatenate(blocks, axis=1), ((0,), (0,)))
    stacked = jnp.concatenate(jnp.split(side_by_side, count, axis=1), axis=0)
    rotated = exact_dot(stacked, base_in, ((1,), (0,)))
    scaled = rotated / jnp.concatenate([divisor] * count, axis=0)
    half = exact_dot(scaled, base_in, ((1,), (1,)))
    side_by_side = jnp.concatenate(jnp.split(half, count, axis=0), axis=1)
    restored = exact_dot(base_out, side_by_side, ((1,), (0,)))
    rows = []
    for q, block in enumerate(jnp.split(restored, count, axis=1)):
        weight = mask_ref[lax.axis_index("doc") * count + q].astype(jnp.float32)
        rows.append(block * weight)
    out_ref[...] = jnp.stack(rows).reshape(count, out_size * in_size).astype(jnp.bfloat16)


def precondition(gradients, basis_in, basis_out, eigen_values, mask):
    vmem, smem = pl.BlockSpec(memory_space=pltpu.VMEM), pl.BlockSpec(memory_space=pltpu.SMEM)
    operands = [
        pltpu.with_memory_space_constraint(a, pltpu.HBM)
        for a in (mask, gradients, basis_in, basis_out, eigen_values)
    ]
    return pl.pallas_call(
        precondition_kernel,
        out_shape=jax.ShapeDtypeStruct(gradients.shape, jnp.bfloat16),
        in_specs=[smem, vmem, vmem, vmem, vmem],
        out_specs=vmem,
        compiler_params=pltpu.CompilerParams(vmem_limit_bytes=4 << 20),
        name="precondition",
    )(*operands)


straight = (
    [(0, 0, h) for h in range(2)]
    + [(0, k, h) for k in (1, 2, 3) for h in range(2)]
    + [(k, 0, h) for k in (1, 2, 3) for h in range(2)]
)
diagonal = (
    [t for i in (1, 3) for t in ((2, i, 0), (2, i, 1), (1, i, 0), (1, i, 1), (3, i, 0))]
    + [(2, 2, 0), (2, 2, 1), (1, 2, 0), (1, 2, 1)]
    + [(3, 2, 0), (3, 2, 1), (3, 1, 1), (3, 3, 1)]
)


def place_kernel(tiles, *refs):
    out_ref = refs[-1]
    doc, layer = lax.axis_index("doc"), lax.axis_index("layer")
    y, x = doc >> 4, (doc >> 2) & 3
    core_row, far_row = (y ^ layer) & 1, (y >> 1) ^ (layer >> 1)
    t = 0
    for piece in refs:
        if t == len(tiles):
            break
        for row in range(0, piece.shape[0], 8):
            ky, kx, half = tiles[t]
            out_ref[core_row ^ (ky & 1), far_row ^ (ky >> 1), x ^ kx, half] = piece[row : row + 8]
            t += 1


def placed(tiles, pieces, flops, begun=None):
    vmem = pl.BlockSpec(memory_space=pltpu.VMEM)
    width = pieces[0].shape[1]
    operands = pieces + ([] if begun is None else [begun])
    return pl.pallas_call(
        functools.partial(place_kernel, tiles),
        out_shape=jax.ShapeDtypeStruct((2, 2, 4, 2, 8, width), jnp.bfloat16),
        in_specs=[vmem] * len(operands),
        out_specs=vmem,
        input_output_aliases={} if begun is None else {len(operands) - 1: 0},
        compiler_params=pltpu.CompilerParams(vmem_limit_bytes=8 << 20),
        cost_estimate=pl.CostEstimate(flops=flops, bytes_accessed=0, transcendentals=0),
        name="placed",
    )(*operands)


def score_kernel(queries_ref, stored_ref, out_ref):
    width = 1024

    def tile(i, carry):
        columns = pl.ds(pl.multiple_of(i * width, width), width)
        out_ref[:, columns] = lax.dot_general(
            queries_ref[...],
            stored_ref[columns, :],
            (((1,), (1,)), ((), ())),
            preferred_element_type=jnp.float32,
        )
        return carry

    lax.fori_loop(0, stored_ref.shape[0] // width, tile, 0)


def score(queries, stored):
    vmem = pl.BlockSpec(memory_space=pltpu.VMEM)
    rows, slots = queries.shape[0], stored.shape[0]
    return pl.pallas_call(
        score_kernel,
        out_shape=jax.ShapeDtypeStruct((rows, slots), jnp.float32),
        in_specs=[vmem, vmem],
        out_specs=vmem,
        compiler_params=pltpu.CompilerParams(vmem_limit_bytes=8 << 20),
        cost_estimate=pl.CostEstimate(
            flops=2 * queries.size * slots, bytes_accessed=0, transcendentals=0
        ),
        name="score",
    )(queries, stored)


def fetch(block, stride, flips=(1, 2, 3)):
    blocks = []
    for k in flips:
        blocks.append(lax.ppermute(block, "doc", doc_pairs(stride, k)))
    return blocks


def ordered(blocks, coordinate):
    low, high = (coordinate & 1) == 1, (coordinate & 2) == 2
    a, b, c, d = blocks
    a, b, c, d = (jnp.where(low, p, q) for p, q in ((b, a), (a, b), (d, c), (c, d)))
    return [jnp.where(high, p, q) for p, q in ((c, a), (d, b), (a, c), (b, d))]


def on_device(query_grads, stored_grads, basis_in, basis_out, eigen_values, layer_mask, doc_counts):
    doc = lax.axis_index("doc")
    z = doc % 4
    stored = pltpu.with_memory_space_constraint(stored_grads[0], pltpu.VMEM)
    own = precondition(
        query_grads[0], basis_in[0], basis_out[0], eigen_values[0], layer_mask[:, 0]
    )

    rows = ordered([own] + fetch(own, 1), z)
    block = lax.optimization_barrier(jnp.concatenate(rows, axis=0))
    along_y, along_x = fetch(block, 16), fetch(block, 4)
    queries = placed(straight, [block] + along_x + along_y, 2 * 10**10)
    (y1, y2, y3), (x1, x2, x3) = along_y, along_x
    upper = jnp.concatenate([y2, y1, y3[:8]])
    lower = jnp.concatenate([x2, x1[8:], x3[8:]])
    diagonals = (
        fetch(upper, 4, (1, 3))
        + fetch(y2, 4, (2,))
        + fetch(x2, 16, (1,))
        + fetch(lower, 16, (3,))
    )
    queries = placed(diagonal, diagonals, 10**8, queries)
    tiles = score(queries.reshape(256, -1), stored)
    tiles = tiles.reshape(2, 2, 4, 2, 8, -1)
    other = lax.ppermute(tiles[1], "layer", layer_pairs(1))
    give = (tiles[0, 1] + other[1]).astype(jnp.bfloat16)
    other_far = lax.ppermute(give, "layer", layer_pairs(2))
    total = tiles[0, 0] + other[0] + other_far.astype(jnp.float32)
    slots = stored.shape[0]
    total = total.reshape(64, slots)
    live_slots = jnp.arange(slots, dtype=jnp.int32) < doc_counts[0]
    return jnp.where(live_slots[None, :], total, jnp.zeros_like(total))


def solution(mesh):
    in_specs = (
        P("layer", "doc", None),
        P("layer", "doc", None),
        P("layer", None, None),
        P("layer", None, None),
        P("layer", None, None),
        P(None, "layer"),
        P("doc"),
    )
    out_specs = P("layer", "doc")
    return jax.shard_map(
        on_device, mesh=mesh, in_specs=in_specs, out_specs=out_specs, check_vma=False
    )
```

```python
import functools

import jax
import jax.numpy as jnp
from jax import lax
from jax.experimental import pallas as pl
from jax.experimental.pallas import tpu as pltpu
from jax.sharding import PartitionSpec as P

damping = 0.1

side = 4


def doc_pairs(stride, flip):
    return [(d, d ^ (flip * stride)) for d in range(side**3)]


def layer_pairs(flip):
    return [(l, l ^ flip) for l in range(4)]


def halves(a):
    high = a.astype(jnp.bfloat16)
    return high, (a - high.astype(jnp.float32)).astype(jnp.bfloat16)


def exact_dot(a, b, dims):
    (a_high, a_low), (b_high, b_low) = halves(a), halves(b)
    dot = lambda p, q: lax.dot_general(p, q, (dims, ((), ())), preferred_element_type=jnp.float32)
    return dot(a_high, b_high) + (dot(a_high, b_low) + dot(a_low, b_high))


def precondition_kernel(mask_ref, grads_ref, basis_in_ref, basis_out_ref, eigen_ref, out_ref):
    count, out_size, in_size = grads_ref.shape[0], basis_out_ref.shape[0], basis_in_ref.shape[0]
    base_in, base_out = basis_in_ref[...], basis_out_ref[...]
    divisor = eigen_ref[...] + damping
    grads = grads_ref[...].astype(jnp.float32).reshape(count, out_size, in_size)
    blocks = [grads[q] for q in range(count)]
    side_by_side = exact_dot(base_out, jnp.concatenate(blocks, axis=1), ((0,), (0,)))
    stacked = jnp.concatenate(jnp.split(side_by_side, count, axis=1), axis=0)
    rotated = exact_dot(stacked, base_in, ((1,), (0,)))
    scaled = rotated / jnp.concatenate([divisor] * count, axis=0)
    half = exact_dot(scaled, base_in, ((1,), (1,)))
    side_by_side = jnp.concatenate(jnp.split(half, count, axis=0), axis=1)
    restored = exact_dot(base_out, side_by_side, ((1,), (0,)))
    rows = []
    for q, block in enumerate(jnp.split(restored, count, axis=1)):
        weight = mask_ref[lax.axis_index("doc") * count + q].astype(jnp.float32)
        rows.append(block * weight)
    out_ref[...] = jnp.stack(rows).reshape(count, out_size * in_size).astype(jnp.bfloat16)


def precondition(gradients, basis_in, basis_out, eigen_values, mask):
    vmem, smem = pl.BlockSpec(memory_space=pltpu.VMEM), pl.BlockSpec(memory_space=pltpu.SMEM)
    operands = [
        pltpu.with_memory_space_constraint(a, pltpu.HBM)
        for a in (mask, gradients, basis_in, basis_out, eigen_values)
    ]
    return pl.pallas_call(
        precondition_kernel,
        out_shape=jax.ShapeDtypeStruct(gradients.shape, jnp.bfloat16),
        in_specs=[smem, vmem, vmem, vmem, vmem],
        out_specs=vmem,
        compiler_params=pltpu.CompilerParams(vmem_limit_bytes=4 << 20),
        name="precondition",
    )(*operands)


straight = (
    [(0, 0, h) for h in range(2)]
    + [(0, k, h) for k in (1, 2, 3) for h in range(2)]
    + [(k, 0, h) for k in (1, 2, 3) for h in range(2)]
)
diagonal = (
    [t for j in (1, 3) for t in ((j, 2, 0), (j, 2, 1), (j, 1, 0), (j, 1, 1), (j, 3, 1))]
    + [(2, 2, 0), (2, 2, 1), (2, 1, 0), (2, 1, 1)]
    + [(2, 3, 0), (2, 3, 1), (1, 3, 0), (3, 3, 0)]
)


def place_kernel(tiles, *refs):
    out_ref = refs[-1]
    doc, layer = lax.axis_index("doc"), lax.axis_index("layer")
    y, x = doc >> 4, (doc >> 2) & 3
    core_row, far_row = (y ^ layer) & 1, (y >> 1) ^ (layer >> 1)
    t = 0
    for piece in refs:
        if t == len(tiles):
            break
        for row in range(0, piece.shape[0], 8):
            ky, kx, half = tiles[t]
            out_ref[core_row ^ (ky & 1), far_row ^ (ky >> 1), x ^ kx, half] = piece[row : row + 8]
            t += 1


def placed(tiles, pieces, flops, begun=None):
    vmem = pl.BlockSpec(memory_space=pltpu.VMEM)
    width = pieces[0].shape[1]
    operands = pieces + ([] if begun is None else [begun])
    return pl.pallas_call(
        functools.partial(place_kernel, tiles),
        out_shape=jax.ShapeDtypeStruct((2, 2, 4, 2, 8, width), jnp.bfloat16),
        in_specs=[vmem] * len(operands),
        out_specs=vmem,
        input_output_aliases={} if begun is None else {len(operands) - 1: 0},
        compiler_params=pltpu.CompilerParams(vmem_limit_bytes=8 << 20),
        cost_estimate=pl.CostEstimate(flops=flops, bytes_accessed=0, transcendentals=0),
        name="placed",
    )(*operands)


def score_kernel(queries_ref, stored_ref, out_ref):
    width = 1024

    def tile(i, carry):
        columns = pl.ds(pl.multiple_of(i * width, width), width)
        out_ref[:, columns] = lax.dot_general(
            queries_ref[...],
            stored_ref[columns, :],
            (((1,), (1,)), ((), ())),
            preferred_element_type=jnp.float32,
        )
        return carry

    lax.fori_loop(0, stored_ref.shape[0] // width, tile, 0)


def score(queries, stored):
    vmem = pl.BlockSpec(memory_space=pltpu.VMEM)
    rows, slots = queries.shape[0], stored.shape[0]
    return pl.pallas_call(
        score_kernel,
        out_shape=jax.ShapeDtypeStruct((rows, slots), jnp.float32),
        in_specs=[vmem, vmem],
        out_specs=vmem,
        compiler_params=pltpu.CompilerParams(vmem_limit_bytes=8 << 20),
        cost_estimate=pl.CostEstimate(
            flops=2 * queries.size * slots, bytes_accessed=0, transcendentals=0
        ),
        name="score",
    )(queries, stored)


def fetch(block, stride, flips=(1, 2, 3)):
    blocks = []
    for k in flips:
        blocks.append(lax.ppermute(block, "doc", doc_pairs(stride, k)))
    return blocks


def ordered(blocks, coordinate):
    low, high = (coordinate & 1) == 1, (coordinate & 2) == 2
    a, b, c, d = blocks
    a, b, c, d = (jnp.where(low, p, q) for p, q in ((b, a), (a, b), (d, c), (c, d)))
    return [jnp.where(high, p, q) for p, q in ((c, a), (d, b), (a, c), (b, d))]


def on_device(query_grads, stored_grads, basis_in, basis_out, eigen_values, layer_mask, doc_counts):
    doc = lax.axis_index("doc")
    z = doc % 4
    stored = pltpu.with_memory_space_constraint(stored_grads[0], pltpu.VMEM)
    own = precondition(
        query_grads[0], basis_in[0], basis_out[0], eigen_values[0], layer_mask[:, 0]
    )

    rows = ordered([own] + fetch(own, 1), z)
    block = lax.optimization_barrier(jnp.concatenate(rows, axis=0))
    along_y, along_x = fetch(block, 16), fetch(block, 4)
    queries = placed(straight, [block] + along_x + along_y, 2 * 10**10)
    (y1, y2, y3), (x1, x2, x3) = along_y, along_x
    upper = jnp.concatenate([y2, y1[:8], y3[:8]])
    lower = jnp.concatenate([x2, x1, x3[8:]])
    diagonals = (
        fetch(lower, 16, (1, 3))
        + fetch(x2, 16, (2,))
        + fetch(y2, 4, (1,))
        + fetch(upper, 4, (3,))
    )
    queries = placed(diagonal, diagonals, 10**8, queries)
    tiles = score(queries.reshape(256, -1), stored)
    tiles = tiles.reshape(2, 2, 4, 2, 8, -1)
    other = lax.ppermute(tiles[1], "layer", layer_pairs(1))
    give = (tiles[0, 1] + other[1]).astype(jnp.bfloat16)
    other_far = lax.ppermute(give, "layer", layer_pairs(2))
    total = tiles[0, 0] + other[0] + other_far.astype(jnp.float32)
    slots = stored.shape[0]
    total = total.reshape(64, slots)
    live_slots = jnp.arange(slots, dtype=jnp.int32) < doc_counts[0]
    return jnp.where(live_slots[None, :], total, jnp.zeros_like(total))


def solution(mesh):
    in_specs = (
        P("layer", "doc", None),
        P("layer", "doc", None),
        P("layer", None, None),
        P("layer", None, None),
        P("layer", None, None),
        P(None, "layer"),
        P("doc"),
    )
    out_specs = P("layer", "doc")
    return jax.shard_map(
        on_device, mesh=mesh, in_specs=in_specs, out_specs=out_specs, check_vma=False
    )
```
